128 devices in a mesh: blk: 8 (over y, z_lo), mode: 16 (over z_hi, x, core).
Axes of the slice: x: 4, y: 4, z: 4 (z_hi: 2, z_lo: 2; z = z_hi * 2 + z_lo), core: 2. Of those that a mesh axis runs over, the one named last changes fastest.
Arguments:
- density: bfloat16 [2, 256, 2048, 256], P(None, 'mode', 'blk'), may hold values from -6 to 6
- kernel_tiles: bfloat16 [256, 16, 8, 2, 128, 128], P('mode', 'blk'), may hold values from -0.125 to 0.125
- tile_index: int32 [256, 16, 8], P('mode', 'blk'), may hold values from 0 to 1
- coupling: bfloat16 [2, 9, 256, 2048], P(None, None, 'mode', 'blk'), may hold values from -4 to 4
- spread: int32 [2048], P('blk'), may hold values from 0 to 4
- liner: int32 [2048], P('blk'), may hold values 0 or 1
Outputs:
- applied: bfloat16 [2, 256, 2048, 256], P(None, 'mode', 'blk')
The draws below stay inside these ranges and needn't reach their ends.
Inputs may be any that keep to these rules, and one draw needn't show every extreme that they name: `tile_index`: each retained tile names one column tile of its source shard.
All inputs are finite; a program needn't handle non-finite values. No bound on the sum of `liner` on one device may be relied on, other than what follows from the above.
Results may differ from the reference program's by a relative error of at most 0.0033.
Values may be sent and summed in bfloat16 or wider, within the bound.
No kernel may reach another device: no remote copies, remote signals or barrier semaphores. Data moves between devices by JAX's collectives and lax.ppermute only.
A program may use at most 320 MiB of HBM per device.

```python
import jax
import jax.numpy as jnp
from jax import lax

MODES = 256
PDEV = 256
POINTS = 2048
TILE = 128
ROWT = 16
RHS = 256
BWMAX = 4
BAND = 9
N_BLK = 8


def plant(drawn, rng, low, top_value):
    shape = drawn.shape
    spot = [jax.random.randint(jax.random.fold_in(rng, axis), (), 0, shape[axis]) for axis in range(len(shape))]
    drawn = drawn.at[tuple(spot)].set(low)
    longest = shape.index(max(shape))
    spot[longest] = (spot[longest] + 1) % shape[longest]
    return drawn.at[tuple(spot)].set(top_value)


def shard_levels(stream_key, extent, cuts, smallest, top_value):
    factor_of = 1.0
    for axis_at, blocks in cuts:
        steps = jax.random.uniform(jax.random.fold_in(jax.random.fold_in(stream_key, 6), axis_at), (blocks,), jnp.float32, smallest / len(cuts), top_value / len(cuts))
        factor_of = factor_of * jnp.repeat(jnp.exp(steps), extent[axis_at] // blocks).reshape((-1,) + (1,) * (len(extent) - 1 - axis_at))
    return factor_of


def gaussian(stream_key, extent, scale, most, pieces=(), held_as=jnp.bfloat16):
    level = shard_levels(stream_key, extent, pieces, -0.22, 0.18) if pieces else 1.0
    result = jax.random.normal(stream_key, extent, jnp.float32) * scale * level
    return jnp.minimum(jnp.maximum(result, -most), most).astype(held_as)


def setup_inputs(seed: int = 0) -> dict:
    keys = jax.random.split(jax.random.key(seed), 7)
    density = gaussian(keys[0], (2, MODES, POINTS, RHS), 1.0, 6.0, ((1, 16), (2, 8)))
    kernel_tiles = gaussian(keys[1], (MODES, ROWT, N_BLK, 2, TILE, TILE), (2 * TILE * N_BLK) ** -0.5, 0.125, ((0, 16), (1, 8)))
    tile_index = plant(jax.random.randint(keys[2], (MODES, ROWT, N_BLK), 0, PDEV // TILE), jax.random.fold_in(keys[2], 1), 0, (PDEV // TILE) - 1).astype(jnp.int32)
    coupling = gaussian(keys[3], (2, BAND, MODES, POINTS), 0.4, 4.0, ((2, 16), (3, 8)))
    spread = plant(jax.random.randint(keys[4], (POINTS,), 0, BWMAX + 1), jax.random.fold_in(keys[4], 1), 0, BWMAX).astype(jnp.int32)
    liner = plant((jax.random.randint(keys[5], (POINTS,), 0, 3) < 1).astype(jnp.int32), jax.random.fold_in(keys[5], 1), 0, 1)
    return {"density": density, "kernel_tiles": kernel_tiles, "tile_index": tile_index, "coupling": coupling, "spread": spread, "liner": liner}


def reference(density, kernel_tiles, tile_index, coupling, spread, liner):
    per_shard = PDEV // TILE
    column_tiles = (jnp.arange(N_BLK, dtype=jnp.int32) * per_shard)[None, None, :] + tile_index
    by_mode = jnp.transpose(density.reshape(2, MODES, POINTS // TILE, TILE, RHS), (1, 0, 2, 3, 4))

    def one_mode(inputs):
        kernel_mode, column_mode, sigma_mode = inputs
        picked = sigma_mode[:, column_mode].astype(jnp.float32)
        kernel_float = kernel_mode.astype(jnp.float32)
        real_part = jnp.einsum("tbqk,tbkr->tqr", kernel_float[:, :, 0], picked[0]) - jnp.einsum("tbqk,tbkr->tqr", kernel_float[:, :, 1], picked[1])
        imag_part = jnp.einsum("tbqk,tbkr->tqr", kernel_float[:, :, 0], picked[1]) + jnp.einsum("tbqk,tbkr->tqr", kernel_float[:, :, 1], picked[0])
        return jnp.stack([real_part, imag_part])

    near_modes = lax.map(one_mode, (kernel_tiles, column_tiles, by_mode))
    near = jnp.transpose(near_modes, (1, 0, 2, 3, 4)).reshape(2, MODES, POINTS, RHS)

    offsets = jnp.abs(jnp.arange(BAND, dtype=jnp.int32) - BWMAX)
    within = (offsets[:, None] <= spread[None, :]) & (liner[None, :] == 1)
    weights = coupling * within[None, :, None, :].astype(jnp.bfloat16)
    padded = jnp.pad(density, ((0, 0), (BWMAX, BWMAX), (0, 0), (0, 0)))
    real_part = jnp.zeros((MODES, POINTS, RHS), jnp.float32)
    imag_part = jnp.zeros((MODES, POINTS, RHS), jnp.float32)
    for offset in range(BAND):
        shifted = padded[:, offset:offset + MODES].astype(jnp.float32)
        weight_now = weights[:, offset].astype(jnp.float32)[..., None]
        real_part = real_part + weight_now[0] * shifted[0] - weight_now[1] * shifted[1]
        imag_part = imag_part + weight_now[0] * shifted[1] + weight_now[1] * shifted[0]
    coupled = jnp.stack([real_part, imag_part]).astype(jnp.bfloat16)
    total = 0.5 * density.astype(jnp.float32) + near + coupled.astype(jnp.float32)
    return total.astype(jnp.bfloat16)
```

```python
import functools

import jax
import jax.numpy as jnp
from jax import lax
from jax.experimental import pallas as pl
from jax.experimental.pallas import tpu as pltpu
from jax.sharding import PartitionSpec as P


TILE = 128
PARTS = ((5, 0, 1, 2, (2, 2, 1)), (5, 1, 2, 0, (2, 2, 1)), (6, 2, 0, 1, (2, 2, 2)))


def blk_of(node):
    gray = node & 3
    return (gray ^ (gray >> 1)) * 2 + (node >> 2)


def node_of(blk):
    y = blk // 2
    return (y ^ (y >> 1)) | ((blk % 2) << 2)


def swap(block, direction):
    pairs = [(blk_of(node), blk_of(node ^ (1 << direction))) for node in range(8)]
    return lax.ppermute(block, "blk", pairs)


def near_rows(index_ref, shard_ref, first, row, kernels, density_refs):
    left, right = [], []
    for slot, density_ref in enumerate(density_refs):
        tile = index_ref[first + row * 8 + shard_ref[slot]]
        at = pl.ds(pl.multiple_of(tile * TILE, TILE), TILE)
        right.append(jnp.concatenate([density_ref[0, 0, at, :], density_ref[1, 0, at, :]], axis=1))
        left.append(kernels(slot, row))
    product = jnp.dot(
        jnp.concatenate(left, axis=1),
        jnp.concatenate(right, axis=0),
        preferred_element_type=jnp.float32,
    )
    width = product.shape[1] // 2
    real_part = product[:TILE, :width] - product[TILE:, width:]
    imag_part = product[:TILE, width:] + product[TILE:, :width]
    return real_part, imag_part


class Steps:
    def __init__(self, starts, offsets, sizes):
        self.starts, self.offsets, self.sizes = starts, offsets, sizes
        self.bounds = [sum(sizes[:at]) for at in range(len(sizes) + 1)]

    def part(self, step):
        return sum((step >= bound).astype(jnp.int32) for bound in self.bounds[1:-1])

    def mode(self, step):
        found = step - self.bounds[0] + self.starts[0] + self.offsets[0]
        for at in range(1, len(self.sizes)):
            here = step - self.bounds[at] + self.starts[at] + self.offsets[at]
            found = jnp.where(step >= self.bounds[at], here, found)
        return found

    def within(self, at, step):
        return jnp.clip(step - self.bounds[at], 0, self.sizes[at] - 1)

    def whole_spec(self, points, rhs):
        return pl.BlockSpec((2, 1, points, rhs), lambda i, *_: (0, self.mode(i), 0, 0))

    def piece_spec(self, at, points, rhs, offset=0):
        return pl.BlockSpec((2, 1, points, rhs), lambda i, *_: (0, offset + self.within(at, i), 0, 0))


def partial_kernel(steps, index0, index1, index2, shard_ref, *refs):
    index_refs, kernel_refs, density_refs, out_refs = (index0, index1, index2), refs[:3], refs[3:15], refs[15:]
    step = pl.program_id(0)
    part = steps.part(step)
    first = steps.mode(step) * 16
    for at in range(3):

        @pl.when(part == at)
        def _(at=at):
            for row in range(2):
                sums = near_rows(
                    index_refs[at], shard_ref.at[pl.ds(4 * at, 4)], first, row,
                    lambda slot, row: kernel_refs[at][0, row, slot].reshape(2 * TILE, TILE),
                    density_refs[4 * at : 4 * at + 4],
                )
                for c in range(2):
                    out_refs[at][c, 0, pl.ds(row * TILE, TILE), :] = sums[c].astype(jnp.bfloat16)


def partial_near(steps, indexes, shard_ids, kernels, densities):
    rows, slots = kernels[0].shape[1:3]
    points, rhs = densities[0].shape[2:]
    count = sum(steps.sizes)
    return pl.pallas_call(
        functools.partial(partial_kernel, steps),
        grid_spec=pltpu.PrefetchScalarGridSpec(
            num_scalar_prefetch=4,
            grid=(count,),
            in_specs=[
                pl.BlockSpec((1, rows, slots, 2, TILE, TILE), lambda i, *_, at=at: (steps.within(at, i), 0, 0, 0, 0, 0))
                for at in range(3)
            ]
            + [steps.piece_spec(at, points, rhs, steps.offsets[at]) for at in range(3) for _ in range(4)],
            out_specs=[steps.piece_spec(at, points, rhs) for at in range(3)],
        ),
        out_shape=[jax.ShapeDtypeStruct((2, size, points, rhs), jnp.bfloat16) for size in steps.sizes],
        cost_estimate=pl.CostEstimate(flops=count * 540_000_000, bytes_accessed=count * 1_900_000, transcendentals=0),
        name="partial_near",
    )(*indexes, shard_ids, *kernels, *densities)


def own_kernel(steps, index_ref, shard_ref, *refs):
    kernel_refs, density_refs, own_ref, coupled_ref, out_ref = refs[:4], refs[4:16], refs[16], refs[17], refs[18]
    step = pl.program_id(0)
    part = steps.part(step)
    first = steps.mode(step) * 16
    for at in range(3):

        @pl.when(part == at)
        def _(at=at):
            for row in range(2):
                sums = near_rows(
                    index_ref, shard_ref.at[pl.ds(4 * at, 4)], first, row,
                    lambda slot, row: kernel_refs[slot][0, row, 0].reshape(2 * TILE, TILE),
                    density_refs[4 * at : 4 * at + 4],
                )
                rows = pl.ds(row * TILE, TILE)
                for c in range(2):
                    total = 0.5 * own_ref[c, 0, rows, :].astype(jnp.float32) + sums[c]
                    out_ref[c, 0, rows, :] = total + coupled_ref[c, 0, rows, :].astype(jnp.float32)


def own_near(steps, index, shard_ids, kernel_tiles, densities, density, coupled):
    rows = kernel_tiles.shape[1]
    points, rhs = density.shape[2:]
    count = sum(steps.sizes)

    def kernel_spec(slot):
        return pl.BlockSpec(
            (1, rows, 1, 2, TILE, TILE),
            lambda i, index_ref, shard_ref: (steps.mode(i), 0, shard_ref[4 * steps.part(i) + slot], 0, 0, 0),
        )

    return pl.pallas_call(
        functools.partial(own_kernel, steps),
        grid_spec=pltpu.PrefetchScalarGridSpec(
            num_scalar_prefetch=2,
            grid=(count,),
            in_specs=[kernel_spec(slot) for slot in range(4)]
            + [steps.piece_spec(at, points, rhs, steps.offsets[at]) for at in range(3) for _ in range(4)]
            + [steps.whole_spec(points, rhs)] * 2,
            out_specs=steps.whole_spec(points, rhs),
        ),
        out_shape=jax.ShapeDtypeStruct(density.shape, jnp.float32),
        cost_estimate=pl.CostEstimate(flops=count * 540_000_000, bytes_accessed=count * 2_600_000, transcendentals=0),
        name="own_near",
    )(index, shard_ids, *([kernel_tiles] * 4), *densities, density, coupled)


def final_kernel(steps, base_ref, o0, o1, o2, *refs):
    out_ref = refs[-1]
    part = steps.part(pl.program_id(0))
    for at, other_ref in enumerate((o0, o1, o2)):

        @pl.when(part == at)
        def _(other_ref=other_ref):
            out_ref[...] = (base_ref[...] + other_ref[...].astype(jnp.float32)).astype(out_ref.dtype)


def final_sum(steps, base, others, running):
    points, rhs = base.shape[2:]
    count = sum(steps.sizes)
    ins = [base, *others] + ([] if running is None else [running])
    return pl.pallas_call(
        functools.partial(final_kernel, steps),
        grid=(count,),
        in_specs=[steps.whole_spec(points, rhs)]
        + [steps.piece_spec(at, points, rhs) for at in range(3)]
        + ([] if running is None else [pl.BlockSpec(memory_space=pl.ANY)]),
        out_specs=steps.whole_spec(points, rhs),
        out_shape=jax.ShapeDtypeStruct(base.shape, jnp.bfloat16),
        input_output_aliases={} if running is None else {4: 0},
        cost_estimate=pl.CostEstimate(flops=count * 262144, bytes_accessed=count * 1_050_000, transcendentals=0),
        name="final_sum",
    )(*ins)


def pack_kernel(chunk_sizes, shard_ref, k0, k1, k2, k3, *out_refs):
    step = pl.program_id(0)
    bound = 0
    for size, out_ref in zip(chunk_sizes, out_refs, strict=True):

        @pl.when((step >= bound) & (step < bound + size))
        def _(out_ref=out_ref):
            for slot, kernel_ref in enumerate((k0, k1, k2, k3)):
                out_ref[:, :, slot] = kernel_ref[:, :, 0]

        bound += size


def pack(steps, chunk_sizes, shard_ids, kernel_tiles):
    rows = kernel_tiles.shape[1]
    count = sum(steps.sizes)

    def kernel_spec(slot):
        return pl.BlockSpec(
            (1, rows, 1, 2, TILE, TILE),
            lambda i, shard_ref: (steps.mode(i), 0, shard_ref[4 * steps.part(i) + slot], 0, 0, 0),
        )

    def out_spec(bound, size):
        return pl.BlockSpec(
            (1, rows, 4, 2, TILE, TILE), lambda i, *_: (jnp.clip(i - bound, 0, size - 1), 0, 0, 0, 0, 0)
        )

    return pl.pallas_call(
        functools.partial(pack_kernel, chunk_sizes),
        grid_spec=pltpu.PrefetchScalarGridSpec(
            num_scalar_prefetch=1,
            grid=(count,),
            in_specs=[kernel_spec(slot) for slot in range(4)],
            out_specs=[out_spec(sum(chunk_sizes[:at]), size) for at, size in enumerate(chunk_sizes)],
        ),
        out_shape=[jax.ShapeDtypeStruct((size, rows, 4, 2, TILE, TILE), jnp.bfloat16) for size in chunk_sizes],
        cost_estimate=pl.CostEstimate(flops=0, bytes_accessed=count * 1_050_000, transcendentals=0),
        name="pack",
    )(shard_ids, *([kernel_tiles] * 4))


def couple_kernel(band, weight_ref, low_ref, own_ref, high_ref, out_ref):
    reach = band // 2
    modes = own_ref.shape[1]

    def window(c, mode):
        if mode < reach:
            return low_ref[c, mode].astype(jnp.float32)
        if mode < reach + modes:
            return own_ref[c, mode - reach].astype(jnp.float32)
        return high_ref[c, mode - reach - modes].astype(jnp.float32)

    shape = own_ref.shape[2:]
    for mode in range(modes):
        real_part = imag_part = None
        for offset in range(band):
            at = offset * modes + mode
            wr = jnp.broadcast_to(weight_ref[:, at : at + 1], shape)
            at += band * modes
            wi = jnp.broadcast_to(weight_ref[:, at : at + 1], shape)
            sr, si = window(0, mode + offset), window(1, mode + offset)
            real_now, imag_now = wr * sr - wi * si, wr * si + wi * sr
            real_part = real_now if real_part is None else real_part + real_now
            imag_part = imag_now if imag_part is None else imag_part + imag_now
        out_ref[0, mode] = real_part.astype(out_ref.dtype)
        out_ref[1, mode] = imag_part.astype(out_ref.dtype)


def couple(density, low, high, weights, rows=16):
    _, modes, points, rhs = density.shape
    band = weights.shape[1]
    reach = band // 2
    by_point = jnp.transpose(weights.astype(jnp.float32).reshape(2 * band * modes, points))

    def spec(count):
        return pl.BlockSpec((2, count, rows, rhs), lambda i: (0, 0, i, 0))

    return pl.pallas_call(
        functools.partial(couple_kernel, band),
        grid=(points // rows,),
        in_specs=[pl.BlockSpec((rows, by_point.shape[1]), lambda i: (i, 0)), spec(reach), spec(modes), spec(reach)],
        out_specs=spec(modes),
        out_shape=jax.ShapeDtypeStruct(density.shape, jnp.bfloat16),
        cost_estimate=pl.CostEstimate(flops=20_000_000_000, bytes_accessed=10_000_000, transcendentals=0),
        name="couple",
    )(by_point, low, density, high)


def apply(density, kernel_tiles, tile_index, coupling, spread, liner):
    band_count = coupling.shape[1]
    reach = band_count // 2
    mode_count = density.shape[1]
    node = node_of(lax.axis_index("blk"))
    starts = [sum(part[0] for part in PARTS[:at]) for at in range(3)]
    all_steps = Steps(starts, [0] * 3, [part[0] for part in PARTS])
    chunk_steps = [
        Steps(starts, [sum(part[4][:chunk]) for part in PARTS], [part[4][chunk] for part in PARTS]) for chunk in range(3)
    ]
    masks = [[0, 1 << one, 1 << two, (1 << one) | (1 << two)] for _, one, two, _, _ in PARTS]
    held = jnp.stack([blk_of(node ^ mask) for part in masks for mask in part])
    theirs = jnp.stack(
        [blk_of(node ^ mask ^ (1 << part[3])) for part, some in zip(PARTS, masks, strict=True) for mask in some]
    )

    own = [lax.slice_in_dim(density, start, start + part[0], axis=1) for start, part in zip(starts, PARTS, strict=True)]
    from_one, from_two, from_both, indexes = [], [], [], []
    for at, part in enumerate(PARTS):
        from_one.append(swap(own[at], part[1]))
    for at, part in enumerate(PARTS):
        from_two.append(swap(own[at], part[2]))
    devices = lax.axis_size("mode")
    forward = [(i, i + 1) for i in range(devices - 1)]
    backward = [(target, source) for source, target in forward]
    low = lax.ppermute(lax.slice_in_dim(density, mode_count - reach, None, axis=1), "mode", forward)
    high = lax.ppermute(lax.slice_in_dim(density, 0, reach, axis=1), "mode", backward)
    index = tile_index.reshape(-1)
    for part in PARTS:
        indexes.append(swap(index, part[3]))
    for at, part in enumerate(PARTS):
        from_both.append(swap(from_one[at], part[2]))
    densities = [ref for at in range(3) for ref in (own[at], from_one[at], from_two[at], from_both[at])]

    leaving = pack(all_steps, [size for part in PARTS for size in part[4]], theirs, kernel_tiles)
    kernels = {}
    for chunk in range(3):
        for at, part in enumerate(PARTS):
            kernels[chunk, at] = swap(leaving[3 * at + chunk], part[3])

    offsets = jnp.abs(jnp.arange(band_count, dtype=jnp.int32) - reach)
    within = (offsets[:, None] <= spread[None, :]) & (liner[None, :] == 1)
    weights = coupling * within[None, :, None, :].astype(jnp.bfloat16)
    coupled = couple(density, low, high, weights)
    base = own_near(all_steps, index, held, kernel_tiles, densities, density, coupled)

    others = {}
    for chunk in range(3):
        sums = partial_near(
            chunk_steps[chunk], indexes, held, [kernels[chunk, at] for at in range(3)], densities
        )
        for at, part in enumerate(PARTS):
            others[chunk, at] = swap(sums[at], part[3])
    running = None
    for chunk in range(3):
        running = final_sum(chunk_steps[chunk], base, [others[chunk, at] for at in range(3)], running)
    return running


def solution(mesh):
    return jax.shard_map(
        apply,
        mesh=mesh,
        in_specs=(
            P(None, "mode", "blk", None),
            P("mode", "blk", None, None, None, None),
            P("mode", "blk", None),
            P(None, None, "mode", "blk"),
            P("blk"),
            P("blk"),
        ),
        out_specs=P(None, "mode", "blk", None),
        check_vma=False,
    )
```

```python
import functools

import jax
import jax.numpy as jnp
from jax import lax
from jax.experimental import pallas as pl
from jax.experimental.pallas import tpu as pltpu
from jax.sharding import PartitionSpec as P


TILE = 128
ROLES = ((0, 1, 2), (1, 2, 0), (2, 0, 1))

GROUPS = (((1,), (1,), (1,)), ((3, 1), (3, 1), (4, 1)))


def blk_of(node):
    gray = node & 3
    return (gray ^ (gray >> 1)) * 2 + (node >> 2)


def node_of(blk):
    y = blk // 2
    return (y ^ (y >> 1)) | ((blk % 2) << 2)


def swap(block, direction):
    pairs = [(blk_of(node), blk_of(node ^ (1 << direction))) for node in range(8)]
    return lax.ppermute(block, "blk", pairs)


def near_rows(index_ref, shard_ref, first, row, kernels, density_refs):
    left, right = [], []
    for slot, density_ref in enumerate(density_refs):
        tile = index_ref[first + row * 8 + shard_ref[slot]]
        at = pl.ds(pl.multiple_of(tile * TILE, TILE), TILE)
        right.append(jnp.concatenate([density_ref[0, 0, at, :], density_ref[1, 0, at, :]], axis=1))
        left.append(kernels(slot, row))
    product = jnp.dot(
        jnp.concatenate(left, axis=1),
        jnp.concatenate(right, axis=0),
        preferred_element_type=jnp.float32,
    )
    width = product.shape[1] // 2
    real_part = product[:TILE, :width] - product[TILE:, width:]
    imag_part = product[:TILE, width:] + product[TILE:, :width]
    return real_part, imag_part


class Steps:
    def __init__(self, starts, offsets, sizes):
        self.starts, self.offsets, self.sizes = starts, offsets, sizes
        self.bounds = [sum(sizes[:at]) for at in range(len(sizes) + 1)]

    def part(self, step):
        return sum((step >= bound).astype(jnp.int32) for bound in self.bounds[1:-1])

    def mode(self, step):
        found = step - self.bounds[0] + self.starts[0] + self.offsets[0]
        for at in range(1, len(self.sizes)):
            here = step - self.bounds[at] + self.starts[at] + self.offsets[at]
            found = jnp.where(step >= self.bounds[at], here, found)
        return found

    def within(self, at, step):
        return jnp.clip(step - self.bounds[at], 0, self.sizes[at] - 1)

    def whole_spec(self, points, rhs, first=0):
        return pl.BlockSpec((2, 1, points, rhs), lambda i, *_: (0, self.mode(i) - first, 0, 0))

    def piece_spec(self, at, points, rhs, offset=0):
        return pl.BlockSpec((2, 1, points, rhs), lambda i, *_: (0, offset + self.within(at, i), 0, 0))


def partial_kernel(steps, index0, index1, index2, shard_ref, *refs):
    index_refs, kernel_refs, density_refs, out_refs = (index0, index1, index2), refs[:3], refs[3:15], refs[15:]
    step = pl.program_id(0)
    part = steps.part(step)
    first = steps.mode(step) * 16
    for at in range(3):

        @pl.when(part == at)
        def _(at=at):
            for row in range(2):
                sums = near_rows(
                    index_refs[at], shard_ref.at[pl.ds(4 * at, 4)], first, row,
                    lambda slot, row: kernel_refs[at][0, row, slot].reshape(2 * TILE, TILE),
                    density_refs[4 * at : 4 * at + 4],
                )
                for c in range(2):
                    out_refs[at][c, 0, pl.ds(row * TILE, TILE), :] = sums[c].astype(jnp.bfloat16)


def partial_near(steps, indexes, shard_ids, kernels, densities):
    rows, slots = kernels[0].shape[1:3]
    points, rhs = densities[0].shape[2:]
    count = sum(steps.sizes)
    return pl.pallas_call(
        functools.partial(partial_kernel, steps),
        grid_spec=pltpu.PrefetchScalarGridSpec(
            num_scalar_prefetch=4,
            grid=(count,),
            in_specs=[
                pl.BlockSpec((1, rows, slots, 2, TILE, TILE), lambda i, *_, at=at: (steps.within(at, i), 0, 0, 0, 0, 0))
                for at in range(3)
            ]
            + [steps.piece_spec(at, points, rhs, steps.offsets[at]) for at in range(3) for _ in range(4)],
            out_specs=[steps.piece_spec(at, points, rhs) for at in range(3)],
        ),
        out_shape=[jax.ShapeDtypeStruct((2, size, points, rhs), jnp.bfloat16) for size in steps.sizes],
        cost_estimate=pl.CostEstimate(flops=count * 540_000_000, bytes_accessed=count * 1_900_000, transcendentals=0),
        name="partial_near",
    )(*indexes, shard_ids, *kernels, *densities)


def own_kernel(steps, index_ref, shard_ref, *refs):
    kernel_refs, density_refs, own_ref, coupled_ref, out_ref = refs[:4], refs[4:16], refs[16], refs[17], refs[18]
    step = pl.program_id(0)
    part = steps.part(step)
    first = steps.mode(step) * 16
    for at in range(3):

        @pl.when(part == at)
        def _(at=at):
            for row in range(2):
                sums = near_rows(
                    index_ref, shard_ref.at[pl.ds(4 * at, 4)], first, row,
                    lambda slot, row: kernel_refs[slot][0, row, 0].reshape(2 * TILE, TILE),
                    density_refs[4 * at : 4 * at + 4],
                )
                rows = pl.ds(row * TILE, TILE)
                for c in range(2):
                    total = 0.5 * own_ref[c, 0, rows, :].astype(jnp.float32) + sums[c]
                    out_ref[c, 0, rows, :] = total + coupled_ref[c, 0, rows, :].astype(jnp.float32)


def own_near(steps, index, shard_ids, kernel_tiles, densities, density, coupled):
    rows = kernel_tiles.shape[1]
    points, rhs = density.shape[2:]
    count = sum(steps.sizes)

    def kernel_spec(slot):
        return pl.BlockSpec(
            (1, rows, 1, 2, TILE, TILE),
            lambda i, index_ref, shard_ref: (steps.mode(i), 0, shard_ref[4 * steps.part(i) + slot], 0, 0, 0),
        )

    return pl.pallas_call(
        functools.partial(own_kernel, steps),
        grid_spec=pltpu.PrefetchScalarGridSpec(
            num_scalar_prefetch=2,
            grid=(count,),
            in_specs=[kernel_spec(slot) for slot in range(4)]
            + [steps.piece_spec(at, points, rhs, steps.offsets[at]) for at in range(3) for _ in range(4)]
            + [steps.whole_spec(points, rhs)] * 2,
            out_specs=steps.whole_spec(points, rhs, steps.starts[0]),
        ),
        out_shape=jax.ShapeDtypeStruct((2, count, points, rhs), jnp.float32),
        cost_estimate=pl.CostEstimate(flops=count * 540_000_000, bytes_accessed=count * 2_600_000, transcendentals=0),
        name="own_near",
    )(index, shard_ids, *([kernel_tiles] * 4), *densities, density, coupled)


def final_kernel(places, base_ref, *refs):
    other_refs, out_ref = refs[: len(refs) - 8], refs[-7]
    base_buf, other_buf, out_buf, base_sem, other_sem, out_sem = refs[-6:]
    reads, writes = [], []
    for slot, (at, offset, inner, mode) in enumerate(places):
        reads.append(
            (
                pltpu.make_async_copy(base_ref.at[:, inner], base_buf.at[slot], base_sem.at[slot]),
                pltpu.make_async_copy(other_refs[at].at[:, offset], other_buf.at[slot], other_sem.at[slot]),
            )
        )
        writes.append(pltpu.make_async_copy(out_buf.at[slot], out_ref.at[:, mode], out_sem.at[slot]))
    for pair in reads:
        for copy in pair:
            copy.start()
    for slot, pair in enumerate(reads):
        for copy in pair:
            copy.wait()
        out_buf[slot] = (base_buf[slot] + other_buf[slot].astype(jnp.float32)).astype(out_buf.dtype)
        writes[slot].start()
    for copy in writes:
        copy.wait()


def final_sum(places, base, others, running):
    points, rhs = base.shape[2:]
    count = len(places)
    here = pl.BlockSpec(memory_space=pl.ANY)
    return pl.pallas_call(
        functools.partial(final_kernel, places),
        in_specs=[here] * (2 + len(others)),
        out_specs=here,
        out_shape=jax.ShapeDtypeStruct(running.shape, running.dtype),
        scratch_shapes=[
            pltpu.VMEM((count, 2, points, rhs), jnp.float32),
            pltpu.VMEM((count, 2, points, rhs), jnp.bfloat16),
            pltpu.VMEM((count, 2, points, rhs), jnp.bfloat16),
            pltpu.SemaphoreType.DMA((count,)),
            pltpu.SemaphoreType.DMA((count,)),
            pltpu.SemaphoreType.DMA((count,)),
        ],
        input_output_aliases={1 + len(others): 0},
        cost_estimate=pl.CostEstimate(flops=count * 262144, bytes_accessed=count * 1_050_000, transcendentals=0),
        name="final_sum",
    )(base, *others, running)


def pack_kernel(chunk_sizes, shard_ref, k0, k1, k2, k3, *out_refs):
    step = pl.program_id(0)
    bound = 0
    for size, out_ref in zip(chunk_sizes, out_refs, strict=True):

        @pl.when((step >= bound) & (step < bound + size))
        def _(out_ref=out_ref):
            for slot, kernel_ref in enumerate((k0, k1, k2, k3)):
                out_ref[:, :, slot] = kernel_ref[:, :, 0]

        bound += size


def pack(steps, chunk_sizes, shard_ids, kernel_tiles):
    rows = kernel_tiles.shape[1]
    count = sum(steps.sizes)

    def kernel_spec(slot):
        return pl.BlockSpec(
            (1, rows, 1, 2, TILE, TILE),
            lambda i, shard_ref: (steps.mode(i), 0, shard_ref[4 * lax.rem(steps.part(i), 3) + slot], 0, 0, 0),
        )

    def out_spec(bound, size):
        return pl.BlockSpec(
            (1, rows, 4, 2, TILE, TILE), lambda i, *_: (jnp.clip(i - bound, 0, size - 1), 0, 0, 0, 0, 0)
        )

    return pl.pallas_call(
        functools.partial(pack_kernel, chunk_sizes),
        grid_spec=pltpu.PrefetchScalarGridSpec(
            num_scalar_prefetch=1,
            grid=(count,),
            in_specs=[kernel_spec(slot) for slot in range(4)],
            out_specs=[out_spec(sum(chunk_sizes[:at]), size) for at, size in enumerate(chunk_sizes)],
        ),
        out_shape=[jax.ShapeDtypeStruct((size, rows, 4, 2, TILE, TILE), jnp.bfloat16) for size in chunk_sizes],
        cost_estimate=pl.CostEstimate(flops=0, bytes_accessed=count * 1_050_000, transcendentals=0),
        name="pack",
    )(shard_ids, *([kernel_tiles] * 4))


def couple_kernel(band, weight_ref, low_ref, own_ref, high_ref, out_ref):
    reach = band // 2
    modes = own_ref.shape[1]

    def window(c, mode):
        if mode < reach:
            return low_ref[c, mode].astype(jnp.float32)
        if mode < reach + modes:
            return own_ref[c, mode - reach].astype(jnp.float32)
        return high_ref[c, mode - reach - modes].astype(jnp.float32)

    shape = own_ref.shape[2:]
    for mode in range(modes):
        real_part = imag_part = None
        for offset in range(band):
            at = offset * modes + mode
            wr = jnp.broadcast_to(weight_ref[:, at : at + 1], shape)
            at += band * modes
            wi = jnp.broadcast_to(weight_ref[:, at : at + 1], shape)
            sr, si = window(0, mode + offset), window(1, mode + offset)
            real_now, imag_now = wr * sr - wi * si, wr * si + wi * sr
            real_part = real_now if real_part is None else real_part + real_now
            imag_part = imag_now if imag_part is None else imag_part + imag_now
        out_ref[0, mode] = real_part.astype(out_ref.dtype)
        out_ref[1, mode] = imag_part.astype(out_ref.dtype)


def couple(density, low, high, weights, rows=16):
    _, modes, points, rhs = density.shape
    band = weights.shape[1]
    reach = band // 2
    by_point = jnp.transpose(weights.astype(jnp.float32).reshape(2 * band * modes, points))

    def spec(count):
        return pl.BlockSpec((2, count, rows, rhs), lambda i: (0, 0, i, 0))

    return pl.pallas_call(
        functools.partial(couple_kernel, band),
        grid=(points // rows,),
        in_specs=[pl.BlockSpec((rows, by_point.shape[1]), lambda i: (i, 0)), spec(reach), spec(modes), spec(reach)],
        out_specs=spec(modes),
        out_shape=jax.ShapeDtypeStruct(density.shape, jnp.bfloat16),
        cost_estimate=pl.CostEstimate(flops=20_000_000_000, bytes_accessed=10_000_000, transcendentals=0),
        name="couple",
    )(by_point, low, density, high)


def apply(density, kernel_tiles, tile_index, coupling, spread, liner):
    band_count = coupling.shape[1]
    reach = band_count // 2
    mode_count = density.shape[1]
    node = node_of(lax.axis_index("blk"))
    sizes = [[sum(chunks) for chunks in group] for group in GROUPS]
    flat = [size for group in sizes for size in group]
    starts = [[sum(flat[: 3 * g + at]) for at in range(3)] for g in range(len(GROUPS))]
    masks = [[0, 1 << one, 1 << two, (1 << one) | (1 << two)] for one, two, _ in ROLES]
    held = jnp.stack([blk_of(node ^ mask) for some in masks for mask in some])
    theirs = jnp.stack(
        [blk_of(node ^ mask ^ (1 << role[2])) for role, some in zip(ROLES, masks, strict=True) for mask in some]
    )

    own, from_one, from_two, from_both = {}, {}, {}, {}
    for g in range(len(GROUPS)):
        for at, role in enumerate(ROLES):
            lo = starts[g][at]
            own[g, at] = lax.slice_in_dim(density, lo, lo + sizes[g][at], axis=1)
            from_one[g, at] = swap(own[g, at], role[0])
            from_two[g, at] = swap(own[g, at], role[1])
            from_both[g, at] = swap(from_one[g, at], role[1])
    devices = lax.axis_size("mode")
    forward = [(i, i + 1) for i in range(devices - 1)]
    backward = [(target, source) for source, target in forward]
    low = lax.ppermute(lax.slice_in_dim(density, mode_count - reach, None, axis=1), "mode", forward)
    high = lax.ppermute(lax.slice_in_dim(density, 0, reach, axis=1), "mode", backward)
    index = tile_index.reshape(-1)
    indexes = []
    for role in ROLES:
        indexes.append(swap(index, role[2]))

    chunks = [
        (g, [group[at][chunk] for at in range(3)], [sum(group[at][:chunk]) for at in range(3)])
        for g, group in reversed(tuple(enumerate(GROUPS)))
        for chunk in range(len(group[0]))
    ]
    packed = pack(
        Steps([start for group in starts for start in group], [0] * len(flat), flat),
        [size for group in GROUPS for some in group for size in some],
        theirs,
        kernel_tiles,
    )
    leaving, taken = {}, 0
    for g, group in enumerate(GROUPS):
        for at in range(3):
            for _ in group[at]:
                leaving.setdefault((g, at), []).append(packed[taken])
                taken += 1
    kernels = {}
    for c, (g, _, _) in enumerate(chunks):
        for at, role in enumerate(ROLES):
            kernels[c, at] = swap(leaving[g, at].pop(0), role[2])

    offsets = jnp.abs(jnp.arange(band_count, dtype=jnp.int32) - reach)
    within = (offsets[:, None] <= spread[None, :]) & (liner[None, :] == 1)
    weights = coupling * within[None, :, None, :].astype(jnp.bfloat16)
    coupled = couple(density, low, high, weights)
    densities = [
        [ref for at in range(3) for ref in (own[g, at], from_one[g, at], from_two[g, at], from_both[g, at])]
        for g in range(len(GROUPS))
    ]
    bases = []
    for g in range(len(GROUPS)):
        steps = Steps(starts[g], [0] * 3, sizes[g])
        bases.append(own_near(steps, index, held, kernel_tiles, densities[g], density, coupled))

    others = {}
    for c, (g, count, offset) in enumerate(chunks):
        sums = partial_near(
            Steps(starts[g], offset, count), indexes, held, [kernels[c, at] for at in range(3)], densities[g]
        )
        for at, role in enumerate(ROLES):
            others[c, at] = swap(sums[at], role[2])
    running = coupled
    for c, (g, count, offset) in enumerate(chunks):
        places = [
            (at, j, starts[g][at] + offset[at] + j - starts[g][0], starts[g][at] + offset[at] + j)
            for at in range(3)
            for j in range(count[at])
        ]
        running = final_sum(places, bases[g], [others[c, at] for at in range(3)], running)
    return running


def solution(mesh):
    return jax.shard_map(
        apply,
        mesh=mesh,
        in_specs=(
            P(None, "mode", "blk", None),
            P("mode", "blk", None, None, None, None),
            P("mode", "blk", None),
            P(None, None, "mode", "blk"),
            P("blk"),
            P("blk"),
        ),
        out_specs=P(None, "mode", "blk", None),
        check_vma=False,
    )
```

```python
import functools

import jax
import jax.numpy as jnp
from jax import lax
from jax.experimental import pallas as pl
from jax.experimental.pallas import tpu as pltpu
from jax.sharding import PartitionSpec as P


TILE = 128
ROLES = ((0, 1, 2), (1, 2, 0), (2, 0, 1))

GROUPS = (((1,), (1,), (1,)), ((2, 2), (2, 2), (3, 2)))


def blk_of(node):
    gray = node & 3
    return (gray ^ (gray >> 1)) * 2 + (node >> 2)


def node_of(blk):
    y = blk // 2
    return (y ^ (y >> 1)) | ((blk % 2) << 2)


def swap(block, direction):
    pairs = [(blk_of(node), blk_of(node ^ (1 << direction))) for node in range(8)]
    return lax.ppermute(block, "blk", pairs)


def near_rows(index_ref, shard_ref, first, row, kernels, density_refs):
    left, right = [], []
    for slot, density_ref in enumerate(density_refs):
        tile = index_ref[first + row * 8 + shard_ref[slot]]
        at = pl.ds(pl.multiple_of(tile * TILE, TILE), TILE)
        right.append(jnp.concatenate([density_ref[0, 0, at, :], density_ref[1, 0, at, :]], axis=1))
        left.append(kernels(slot, row))
    product = jnp.dot(
        jnp.concatenate(left, axis=1),
        jnp.concatenate(right, axis=0),
        preferred_element_type=jnp.float32,
    )
    width = product.shape[1] // 2
    real_part = product[:TILE, :width] - product[TILE:, width:]
    imag_part = product[:TILE, width:] + product[TILE:, :width]
    return real_part, imag_part


class Steps:
    def __init__(self, starts, offsets, sizes):
        self.starts, self.offsets, self.sizes = starts, offsets, sizes
        self.bounds = [sum(sizes[:at]) for at in range(len(sizes) + 1)]

    def part(self, step):
        return sum((step >= bound).astype(jnp.int32) for bound in self.bounds[1:-1])

    def mode(self, step):
        found = step - self.bounds[0] + self.starts[0] + self.offsets[0]
        for at in range(1, len(self.sizes)):
            here = step - self.bounds[at] + self.starts[at] + self.offsets[at]
            found = jnp.where(step >= self.bounds[at], here, found)
        return found

    def within(self, at, step):
        return jnp.clip(step - self.bounds[at], 0, self.sizes[at] - 1)

    def whole_spec(self, points, rhs, first=0):
        return pl.BlockSpec((2, 1, points, rhs), lambda i, *_: (0, self.mode(i) - first, 0, 0))

    def piece_spec(self, at, points, rhs, offset=0):
        return pl.BlockSpec((2, 1, points, rhs), lambda i, *_: (0, offset + self.within(at, i), 0, 0))


def partial_kernel(steps, index0, index1, index2, shard_ref, *refs):
    index_refs, kernel_refs, density_refs, out_refs = (index0, index1, index2), refs[:3], refs[3:15], refs[15:]
    step = pl.program_id(0)
    part = steps.part(step)
    first = steps.mode(step) * 16
    for at in range(3):

        @pl.when(part == at)
        def _(at=at):
            for row in range(2):
                sums = near_rows(
                    index_refs[at], shard_ref.at[pl.ds(4 * at, 4)], first, row,
                    lambda slot, row: kernel_refs[at][0, row, slot].reshape(2 * TILE, TILE),
                    density_refs[4 * at : 4 * at + 4],
                )
                for c in range(2):
                    out_refs[at][c, 0, pl.ds(row * TILE, TILE), :] = sums[c].astype(jnp.bfloat16)


def partial_near(steps, indexes, shard_ids, kernels, densities):
    rows, slots = kernels[0].shape[1:3]
    points, rhs = densities[0].shape[2:]
    count = sum(steps.sizes)
    return pl.pallas_call(
        functools.partial(partial_kernel, steps),
        grid_spec=pltpu.PrefetchScalarGridSpec(
            num_scalar_prefetch=4,
            grid=(count,),
            in_specs=[
                pl.BlockSpec((1, rows, slots, 2, TILE, TILE), lambda i, *_, at=at: (steps.within(at, i), 0, 0, 0, 0, 0))
                for at in range(3)
            ]
            + [steps.piece_spec(at, points, rhs, steps.offsets[at]) for at in range(3) for _ in range(4)],
            out_specs=[steps.piece_spec(at, points, rhs) for at in range(3)],
        ),
        out_shape=[jax.ShapeDtypeStruct((2, size, points, rhs), jnp.bfloat16) for size in steps.sizes],
        cost_estimate=pl.CostEstimate(flops=count * 540_000_000, bytes_accessed=count * 1_900_000, transcendentals=0),
        name="partial_near",
    )(*indexes, shard_ids, *kernels, *densities)


def own_kernel(steps, index_ref, shard_ref, *refs):
    kernel_refs, density_refs, own_ref, coupled_ref, out_ref = refs[:4], refs[4:16], refs[16], refs[17], refs[18]
    step = pl.program_id(0)
    part = steps.part(step)
    first = steps.mode(step) * 16
    for at in range(3):

        @pl.when(part == at)
        def _(at=at):
            for row in range(2):
                sums = near_rows(
                    index_ref, shard_ref.at[pl.ds(4 * at, 4)], first, row,
                    lambda slot, row: kernel_refs[slot][0, row, 0].reshape(2 * TILE, TILE),
                    density_refs[4 * at : 4 * at + 4],
                )
                rows = pl.ds(row * TILE, TILE)
                for c in range(2):
                    total = 0.5 * own_ref[c, 0, rows, :].astype(jnp.float32) + sums[c]
                    out_ref[c, 0, rows, :] = total + coupled_ref[c, 0, rows, :].astype(jnp.float32)


def own_near(steps, index, shard_ids, kernel_tiles, densities, density, coupled):
    rows = kernel_tiles.shape[1]
    points, rhs = density.shape[2:]
    count = sum(steps.sizes)

    def kernel_spec(slot):
        return pl.BlockSpec(
            (1, rows, 1, 2, TILE, TILE),
            lambda i, index_ref, shard_ref: (steps.mode(i), 0, shard_ref[4 * steps.part(i) + slot], 0, 0, 0),
        )

    return pl.pallas_call(
        functools.partial(own_kernel, steps),
        grid_spec=pltpu.PrefetchScalarGridSpec(
            num_scalar_prefetch=2,
            grid=(count,),
            in_specs=[kernel_spec(slot) for slot in range(4)]
            + [steps.piece_spec(at, points, rhs, steps.offsets[at]) for at in range(3) for _ in range(4)]
            + [steps.whole_spec(points, rhs)] * 2,
            out_specs=steps.whole_spec(points, rhs, steps.starts[0]),
        ),
        out_shape=jax.ShapeDtypeStruct((2, count, points, rhs), jnp.float32),
        cost_estimate=pl.CostEstimate(flops=count * 540_000_000, bytes_accessed=count * 2_600_000, transcendentals=0),
        name="own_near",
    )(index, shard_ids, *([kernel_tiles] * 4), *densities, density, coupled)


def final_kernel(places, base_ref, *refs):
    other_refs, out_ref = refs[: len(refs) - 8], refs[-7]
    base_buf, other_buf, out_buf, base_sem, other_sem, out_sem = refs[-6:]
    reads, writes = [], []
    for slot, (at, offset, inner, mode) in enumerate(place for place in places for _ in range(2)):
        place, c = slot // 2, slot % 2
        reads.append(
            (
                pltpu.make_async_copy(base_ref.at[c, inner], base_buf.at[place, c], base_sem.at[slot]),
                pltpu.make_async_copy(other_refs[at].at[c, offset], other_buf.at[place, c], other_sem.at[slot]),
            )
        )
        writes.append(pltpu.make_async_copy(out_buf.at[place, c], out_ref.at[c, mode], out_sem.at[slot]))
    for pair in reads:
        for copy in pair:
            copy.start()
    for slot, pair in enumerate(reads):
        for copy in pair:
            copy.wait()
        place, c = slot // 2, slot % 2
        total = base_buf[place, c] + other_buf[place, c].astype(jnp.float32)
        out_buf[place, c] = total.astype(out_buf.dtype)
        writes[slot].start()
    for copy in writes:
        copy.wait()


def final_sum(places, base, others, running):
    points, rhs = base.shape[2:]
    count = len(places)
    here = pl.BlockSpec(memory_space=pl.ANY)
    return pl.pallas_call(
        functools.partial(final_kernel, places),
        in_specs=[here] * (2 + len(others)),
        out_specs=here,
        out_shape=jax.ShapeDtypeStruct(running.shape, running.dtype),
        scratch_shapes=[
            pltpu.VMEM((count, 2, points, rhs), jnp.float32),
            pltpu.VMEM((count, 2, points, rhs), jnp.bfloat16),
            pltpu.VMEM((count, 2, points, rhs), jnp.bfloat16),
            pltpu.SemaphoreType.DMA((2 * count,)),
            pltpu.SemaphoreType.DMA((2 * count,)),
            pltpu.SemaphoreType.DMA((2 * count,)),
        ],
        input_output_aliases={1 + len(others): 0},
        cost_estimate=pl.CostEstimate(flops=count * 262144, bytes_accessed=count * 1_050_000, transcendentals=0),
        name="final_sum",
    )(base, *others, running)


def pack_kernel(chunk_sizes, shard_ref, k0, k1, k2, k3, *out_refs):
    step = pl.program_id(0)
    bound = 0
    for size, out_ref in zip(chunk_sizes, out_refs, strict=True):

        @pl.when((step >= bound) & (step < bound + size))
        def _(out_ref=out_ref):
            for slot, kernel_ref in enumerate((k0, k1, k2, k3)):
                out_ref[:, :, slot] = kernel_ref[:, :, 0]

        bound += size


def pack(steps, chunk_sizes, shard_ids, kernel_tiles):
    rows = kernel_tiles.shape[1]
    count = sum(steps.sizes)

    def kernel_spec(slot):
        return pl.BlockSpec(
            (1, rows, 1, 2, TILE, TILE),
            lambda i, shard_ref: (steps.mode(i), 0, shard_ref[4 * lax.rem(steps.part(i), 3) + slot], 0, 0, 0),
        )

    def out_spec(bound, size):
        return pl.BlockSpec(
            (1, rows, 4, 2, TILE, TILE), lambda i, *_: (jnp.clip(i - bound, 0, size - 1), 0, 0, 0, 0, 0)
        )

    return pl.pallas_call(
        functools.partial(pack_kernel, chunk_sizes),
        grid_spec=pltpu.PrefetchScalarGridSpec(
            num_scalar_prefetch=1,
            grid=(count,),
            in_specs=[kernel_spec(slot) for slot in range(4)],
            out_specs=[out_spec(sum(chunk_sizes[:at]), size) for at, size in enumerate(chunk_sizes)],
        ),
        out_shape=[jax.ShapeDtypeStruct((size, rows, 4, 2, TILE, TILE), jnp.bfloat16) for size in chunk_sizes],
        cost_estimate=pl.CostEstimate(flops=0, bytes_accessed=count * 1_050_000, transcendentals=0),
        name="pack",
    )(shard_ids, *([kernel_tiles] * 4))


def couple_kernel(band, weight_ref, low_ref, own_ref, high_ref, out_ref):
    reach = band // 2
    modes = own_ref.shape[1]

    def window(c, mode):
        if mode < reach:
            return low_ref[c, mode].astype(jnp.float32)
        if mode < reach + modes:
            return own_ref[c, mode - reach].astype(jnp.float32)
        return high_ref[c, mode - reach - modes].astype(jnp.float32)

    shape = own_ref.shape[2:]
    for mode in range(modes):
        real_part = imag_part = None
        for offset in range(band):
            at = offset * modes + mode
            wr = jnp.broadcast_to(weight_ref[:, at : at + 1], shape)
            at += band * modes
            wi = jnp.broadcast_to(weight_ref[:, at : at + 1], shape)
            sr, si = window(0, mode + offset), window(1, mode + offset)
            real_now, imag_now = wr * sr - wi * si, wr * si + wi * sr
            real_part = real_now if real_part is None else real_part + real_now
            imag_part = imag_now if imag_part is None else imag_part + imag_now
        out_ref[0, mode] = real_part.astype(out_ref.dtype)
        out_ref[1, mode] = imag_part.astype(out_ref.dtype)


def couple(density, low, high, weights, rows=16):
    _, modes, points, rhs = density.shape
    band = weights.shape[1]
    reach = band // 2
    by_point = jnp.transpose(weights.astype(jnp.float32).reshape(2 * band * modes, points))

    def spec(count):
        return pl.BlockSpec((2, count, rows, rhs), lambda i: (0, 0, i, 0))

    return pl.pallas_call(
        functools.partial(couple_kernel, band),
        grid=(points // rows,),
        in_specs=[pl.BlockSpec((rows, by_point.shape[1]), lambda i: (i, 0)), spec(reach), spec(modes), spec(reach)],
        out_specs=spec(modes),
        out_shape=jax.ShapeDtypeStruct(density.shape, jnp.bfloat16),
        cost_estimate=pl.CostEstimate(flops=20_000_000_000, bytes_accessed=10_000_000, transcendentals=0),
        name="couple",
    )(by_point, low, density, high)


def apply(density, kernel_tiles, tile_index, coupling, spread, liner):
    band_count = coupling.shape[1]
    reach = band_count // 2
    mode_count = density.shape[1]
    node = node_of(lax.axis_index("blk"))
    sizes = [[sum(chunks) for chunks in group] for group in GROUPS]
    flat = [size for group in sizes for size in group]
    starts = [[sum(flat[: 3 * g + at]) for at in range(3)] for g in range(len(GROUPS))]
    masks = [[0, 1 << one, 1 << two, (1 << one) | (1 << two)] for one, two, _ in ROLES]
    held = jnp.stack([blk_of(node ^ mask) for some in masks for mask in some])
    theirs = jnp.stack(
        [blk_of(node ^ mask ^ (1 << role[2])) for role, some in zip(ROLES, masks, strict=True) for mask in some]
    )

    own, from_one, from_two, from_both = {}, {}, {}, {}
    for g in range(len(GROUPS)):
        for at, role in enumerate(ROLES):
            lo = starts[g][at]
            own[g, at] = lax.slice_in_dim(density, lo, lo + sizes[g][at], axis=1)
            from_one[g, at] = swap(own[g, at], role[0])
            from_two[g, at] = swap(own[g, at], role[1])
            from_both[g, at] = swap(from_one[g, at], role[1])
    devices = lax.axis_size("mode")
    forward = [(i, i + 1) for i in range(devices - 1)]
    backward = [(target, source) for source, target in forward]
    low = lax.ppermute(lax.slice_in_dim(density, mode_count - reach, None, axis=1), "mode", forward)
    high = lax.ppermute(lax.slice_in_dim(density, 0, reach, axis=1), "mode", backward)
    index = tile_index.reshape(-1)
    indexes = []
    for role in ROLES:
        indexes.append(swap(index, role[2]))

    chunks = [
        (g, [group[at][chunk] for at in range(3)], [sum(group[at][:chunk]) for at in range(3)])
        for g, group in reversed(tuple(enumerate(GROUPS)))
        for chunk in range(len(group[0]))
    ]
    packed = pack(
        Steps([start for group in starts for start in group], [0] * len(flat), flat),
        [size for group in GROUPS for some in group for size in some],
        theirs,
        kernel_tiles,
    )
    leaving, taken = {}, 0
    for g, group in enumerate(GROUPS):
        for at in range(3):
            for _ in group[at]:
                leaving.setdefault((g, at), []).append(packed[taken])
                taken += 1
    kernels = {}
    for c, (g, _, _) in enumerate(chunks):
        for at, role in enumerate(ROLES):
            kernels[c, at] = swap(leaving[g, at].pop(0), role[2])

    offsets = jnp.abs(jnp.arange(band_count, dtype=jnp.int32) - reach)
    within = (offsets[:, None] <= spread[None, :]) & (liner[None, :] == 1)
    weights = coupling * within[None, :, None, :].astype(jnp.bfloat16)
    coupled = couple(density, low, high, weights)
    densities = [
        [ref for at in range(3) for ref in (own[g, at], from_one[g, at], from_two[g, at], from_both[g, at])]
        for g in range(len(GROUPS))
    ]
    bases = []
    for g in range(len(GROUPS)):
        steps = Steps(starts[g], [0] * 3, sizes[g])
        bases.append(own_near(steps, index, held, kernel_tiles, densities[g], density, coupled))

    others = {}
    for c, (g, count, offset) in enumerate(chunks):
        sums = partial_near(
            Steps(starts[g], offset, count), indexes, held, [kernels[c, at] for at in range(3)], densities[g]
        )
        for at, role in enumerate(ROLES):
            others[c, at] = swap(sums[at], role[2])
    running = coupled
    for c, (g, count, offset) in enumerate(chunks):
        places = [
            (at, j, starts[g][at] + offset[at] + j - starts[g][0], starts[g][at] + offset[at] + j)
            for at in range(3)
            for j in range(count[at])
        ]
        running = final_sum(places, bases[g], [others[c, at] for at in range(3)], running)
    return running


def solution(mesh):
    return jax.shard_map(
        apply,
        mesh=mesh,
        in_specs=(
            P(None, "mode", "blk", None),
            P("mode", "blk", None, None, None, None),
            P("mode", "blk", None),
            P(None, None, "mode", "blk"),
            P("blk"),
            P("blk"),
        ),
        out_specs=P(None, "mode", "blk", None),
        check_vma=False,
    )
```
